32 devices in a mesh: beam: 2 (over x), freq: 16 (over z, y, core).
Axes of the slice: x: 2, y: 2, z: 4, core: 2. Of those that a mesh axis runs over, the one named last changes fastest.
Arguments:
- spectrum: bfloat16 [2, 65536], P(None, ('beam', 'freq')), parts along dimension 1, may hold values from -6 to 6
- template_bank: bfloat16 [2, 256, 1024], replicated, may hold values from -0.125 to 0.125
- template_index: int32 [128], replicated, may hold values from 0 to 255
Outputs:
- harmonic_sum: float32 [128, 65536], P(None, ('beam', 'freq')), parts along dimension 1
The draws below stay inside these ranges and needn't reach their ends.
There are 2 independent parts, one for each index of `beam`. The reference program is written for one: setup_inputs(seed, part) draws one part's arguments, and reference() takes and returns one part's arrays. A program takes and returns all parts, laid end to end along the dimension named above; an argument that names none is the same for every part. Nothing has to cross between parts.
Inputs may be any that keep to these rules, and one draw needn't show every extreme that they name: `template_index`: entry z names the bank template of acceleration row z.
All inputs are finite; a program needn't handle non-finite values.
Results may differ from the reference program's by a relative error of at most 0.002.
Values may be sent and summed in bfloat16 or wider, within the bound.
A program may use at most 64 MiB of HBM per device.

```python
import jax
import jax.numpy as jnp
from jax import lax

ZROWS = 128
TAPS = 1024
NBANK = 256
BINS = 32768


def set_ends(array, stream_key, smallest, largest):
    shape = array.shape
    spot = [jax.random.randint(jax.random.fold_in(stream_key, axis), (), 0, shape[axis]) for axis in range(len(shape))]
    array = array.at[tuple(spot)].set(smallest)
    longest = shape.index(max(shape))
    spot[longest] = (spot[longest] + 1) % shape[longest]
    return array.at[tuple(spot)].set(largest)


def shard_levels(rng, shape, pieces, low, high):
    factor_of, own = 1.0, jax.random.fold_in(rng, 6)
    for dim, shards_of in pieces:
        draws = jnp.exp(jax.random.uniform(jax.random.fold_in(own, dim), (shards_of,), jnp.float32, low / len(pieces), high / len(pieces)))
        factor_of = factor_of * jnp.repeat(draws, shape[dim] // shards_of).reshape([-1 if axis == dim else 1 for axis in range(len(shape))])
    return factor_of


def bell_draw(stream_key, shape, spread, limit, cuts=(), kind=jnp.bfloat16):
    values = spread * jax.random.normal(stream_key, shape, jnp.float32)
    if cuts:
        values = values * shard_levels(stream_key, shape, cuts, -0.22, 0.18)
    return jnp.clip(values, -limit, limit).astype(kind)


def setup_inputs(seed: int = 0, part: int = 0) -> dict:
    key_of = jax.random.split(jax.random.key(seed), 4)
    part_splits = jax.random.split(jax.random.fold_in(key_of[3], part), 4)
    return {
        "spectrum": bell_draw(part_splits[0], (2, BINS), 1.0, 6.0, ((1, 16),)),
        "template_bank": bell_draw(key_of[1], (2, NBANK, TAPS), (2 * TAPS) ** -0.5, 0.125),
        "template_index": set_ends(jax.random.randint(key_of[2], (ZROWS,), 0, NBANK), jax.random.fold_in(key_of[2], 1), 0, NBANK - 1).astype(jnp.int32),
    }


def reference(spectrum, template_bank, template_index):
    half_taps = TAPS // 2
    length_fft = 2 * BINS
    template_re = template_bank[0][template_index].astype(jnp.float32)
    template_im = template_bank[1][template_index].astype(jnp.float32)
    signal = lax.complex(spectrum[0].astype(jnp.float32), spectrum[1].astype(jnp.float32))
    padded = jnp.pad(signal, (half_taps, length_fft - BINS - half_taps))
    signal_freq = jnp.fft.fft(padded)

    def correlate_row(pair):
        row_re, row_im = pair
        row = lax.complex(row_re, row_im)
        row_pad = jnp.pad(row, (0, length_fft - TAPS))
        kernel_freq = jnp.conj(jnp.fft.fft(jnp.conj(row_pad)))
        correlated = jnp.fft.ifft(signal_freq * kernel_freq)[:BINS]
        real_part = jnp.real(correlated)
        imag_part = jnp.imag(correlated)
        return (real_part * real_part + imag_part * imag_part).astype(jnp.bfloat16)

    plane = lax.map(correlate_row, (template_re, template_im))
    total = plane.astype(jnp.float32)
    for numerator, denominator in ((1, 2), (1, 4), (3, 4)):
        row_index = (jnp.arange(ZROWS, dtype=jnp.int32) * numerator) // denominator
        col_index = (jnp.arange(BINS, dtype=jnp.int32) * numerator) // denominator
        total = total + plane[row_index][:, col_index].astype(jnp.float32)
    return total
```

```python
import functools

import jax
import jax.numpy as jnp
from jax import lax
from jax.experimental import pallas as pl
from jax.experimental.pallas import tpu as pltpu
from jax.sharding import PartitionSpec as P

RATIOS = ((1, 1), (1, 2), (1, 4), (3, 4))
CHUNK = 256
LANES = 128


class Plan:
    def __init__(self, cols, taps, rows, owners):
        self.cols, self.taps, self.rows, self.owners = cols, taps, rows, owners
        self.granule = taps // 2
        self.held = cols // self.granule
        self.steps = [self.held * n // d for n, d in RATIOS]
        self.part_cols = [cols * n // d for n, d in RATIOS]
        self.part_rows = [rows * n // d for n, d in RATIOS]
        self.offsets, self.slots = [], []
        offset = slot = 0
        for width in self.part_cols:
            self.offsets.append(offset)
            self.slots.append(slot)
            offset += width + taps
            slot += (width + taps) // self.granule
        self.width, self.slot_count = offset, slot


def sends(plan, me):
    found = []
    for own in range(plan.held):
        for part, step in enumerate(plan.steps):
            spot = plan.held * me + own + 1
            last = spot // step
            rest = spot - last * step
            for back in range((step + 1) // step + 1):
                if plan.held % step == 0:
                    if (own + 1) % step + step * back >= step + 2:
                        continue
                to = last - back
                place = rest + step * back
                fits = (to >= 0) & (to < plan.owners) & (place < step + 2)
                found.append((own, part, to, place, fits))
    return found


def gather_kernel(plan, spec_ref, index_ref, bank_ref, win_ref, lhs_ref, bank, bank_sem, send_sems, recv_sems):
    me = lax.axis_index("freq")
    size = plan.granule
    rows = plan.rows
    fetch = pltpu.make_async_copy(bank_ref, bank, bank_sem)
    fetch.start()
    barrier = pltpu.get_barrier_semaphore()

    def greet(step, carry):
        peer = lax.rem(me + step, plan.owners)
        pl.semaphore_signal(barrier, inc=1, device_id={"freq": peer}, device_id_type=pl.DeviceIdType.MESH)
        return carry

    lax.fori_loop(1, plan.owners, greet, 0)

    @pl.when(me == 0)
    def _():
        for offset in plan.offsets:
            win_ref[:, offset : offset + size] = jnp.zeros((2, size), win_ref.dtype)

    @pl.when(me == plan.owners - 1)
    def _():
        end = plan.offsets[0] + plan.part_cols[0] + plan.taps
        win_ref[:, end - size : end] = jnp.zeros((2, size), win_ref.dtype)

    pl.semaphore_wait(barrier, plan.owners - 1)

    def each(act_remote, act_local):
        for number, (own, part, to, place, fits) in enumerate(sends(plan, me)):
            source = spec_ref.at[:, own * size : (own + 1) * size]
            target = win_ref.at[:, pl.ds(pl.multiple_of(plan.offsets[part] + place * size, size), size)]
            got = recv_sems.at[plan.slots[part] + place]

            @pl.when(fits & (to != me))
            def _():
                act_remote(
                    pltpu.make_async_remote_copy(
                        src_ref=source,
                        dst_ref=target,
                        send_sem=send_sems.at[number],
                        recv_sem=got,
                        device_id={"freq": to},
                        device_id_type=pl.DeviceIdType.MESH,
                    )
                )

            if act_local is not None:

                @pl.when(fits & (to == me))
                def _():
                    act_local(pltpu.make_async_copy(source, target, got))

    each(lambda copy: copy.start(), lambda copy: copy.start())

    fetch.wait()
    names = lax.broadcasted_iota(jnp.int32, (bank.shape[1], rows), 0)
    picks = (names == index_ref[...]).astype(jnp.float32).T.astype(jnp.bfloat16)
    real = jnp.dot(picks, bank[0], preferred_element_type=jnp.float32).astype(jnp.bfloat16)
    imag = jnp.dot(picks, bank[1], preferred_element_type=jnp.float32).astype(jnp.bfloat16)
    lhs_ref[0, :rows] = real
    lhs_ref[0, rows:] = imag
    lhs_ref[1, :rows] = -imag
    lhs_ref[1, rows:] = real

    for part, step in enumerate(plan.steps):
        for place in range(step + 2):
            spot = step * me - 1 + place

            @pl.when((spot >= 0) & (spot < plan.held * plan.owners))
            def _():
                start = plan.offsets[part] + place * size
                pltpu.make_async_copy(
                    spec_ref.at[:, 0:size],
                    win_ref.at[:, start : start + size],
                    recv_sems.at[plan.slots[part] + place],
                ).wait()

    each(lambda copy: copy.wait_send(), None)


def one_hot(shape, make):
    left = lax.broadcasted_iota(jnp.int32, shape, 0)
    right = lax.broadcasted_iota(jnp.int32, shape, 1)
    return make(left, right).astype(jnp.float32).astype(jnp.bfloat16)


def search_kernel(plan, win_ref, lhs_ref, out_ref, shifts_re, shifts_im, half_ref, quarter_ref, three_ref):
    rows, taps = plan.rows, plan.taps
    width = plan.width
    blocks = width // LANES

    for which, shifts in ((0, shifts_re), (1, shifts_im)):
        base = jnp.broadcast_to(win_ref[which : which + 1, :].astype(jnp.float32), (16, width))
        place = lax.broadcasted_iota(jnp.int32, (16, width), 0)
        for bit in (1, 2, 4, 8):
            base = jnp.where((place & bit) != 0, pltpu.roll(base, width - bit, 1), base)
        base = base.astype(jnp.bfloat16)
        for turn in range(LANES // 16):
            moved = base if turn == 0 else pltpu.roll(base, width - 16 * turn, 1)
            for block in range(blocks):
                piece = moved[:, block * LANES : (block + 1) * LANES]
                spot = block * LANES + 16 * turn
                shifts[spot : spot + 16, 0:LANES] = piece
                if block:
                    shifts[spot - LANES : spot - LANES + 16, LANES : 2 * LANES] = piece

    def power(part, chunk):
        count = plan.part_rows[part]
        start = pl.multiple_of(plan.offsets[part] + chunk * CHUNK, CHUNK)

        def left(which):
            if count == rows:
                return lhs_ref[which]
            return jnp.concatenate([lhs_ref[which, :count], lhs_ref[which, rows : rows + count]], 0)

        both = jnp.dot(left(0), shifts_re[pl.ds(start, taps), :], preferred_element_type=jnp.float32)
        both += jnp.dot(left(1), shifts_im[pl.ds(start, taps), :], preferred_element_type=jnp.float32)
        real, imag = both[:count], both[count:]
        return (real * real + imag * imag).astype(jnp.bfloat16)

    for part, held in ((1, half_ref), (2, quarter_ref), (3, three_ref)):
        n, d = RATIOS[part]
        spread = one_hot((rows, plan.part_rows[part]), lambda z, k: z * n // d == k)

        def fill(chunk, carry):
            cells = jnp.dot(spread, power(part, chunk), preferred_element_type=jnp.float32)
            held[:, pl.ds(pl.multiple_of(chunk * CHUNK, CHUNK), CHUNK)] = cells.astype(jnp.bfloat16)
            return carry

        lax.fori_loop(0, plan.part_cols[part] // CHUNK, fill, 0)

    half = one_hot((LANES, CHUNK), lambda k, r: k == r // 2)
    quarters = [one_hot((LANES, CHUNK), lambda k, r: k == CHUNK // 4 * odd + r // 4) for odd in (0, 1)]
    threes = [one_hot((CHUNK, CHUNK), lambda k, r: k == CHUNK // 4 * odd + 3 * r // 4) for odd in (0, 1)]
    spreads = [jnp.concatenate([half, quarters[odd], threes[odd]], 0) for odd in (0, 1)]

    def pair(step, carry):
        for odd in (0, 1):
            chunk = 2 * step + odd
            total = power(0, chunk).astype(jnp.float32)
            cells = jnp.concatenate(
                [
                    half_ref[:, pl.ds(pl.multiple_of(chunk * LANES, LANES), LANES)],
                    quarter_ref[:, pl.ds(pl.multiple_of(step * LANES, LANES), LANES)],
                    three_ref[:, pl.ds(pl.multiple_of(step * 3 * LANES + odd * LANES, LANES), CHUNK)],
                ],
                1,
            )
            total += jnp.dot(cells, spreads[odd], preferred_element_type=jnp.float32)
            out_ref[:, pl.ds(pl.multiple_of(chunk * CHUNK, CHUNK), CHUNK)] = total
        return carry

    lax.fori_loop(0, plan.cols // (2 * CHUNK), pair, 0)


def body(spectrum, template_bank, template_index):
    owners = lax.axis_size("freq")
    bank_count, taps = template_bank.shape[1:]
    rows = template_index.shape[0]
    cols = spectrum.shape[1]
    plan = Plan(cols, taps, rows, owners)
    send_count = len(sends(plan, 0))
    vmem = pl.BlockSpec(memory_space=pltpu.VMEM)
    windows, lhs = pl.pallas_call(
        functools.partial(gather_kernel, plan),
        out_shape=(
            jax.ShapeDtypeStruct((2, plan.width), jnp.bfloat16),
            jax.ShapeDtypeStruct((2, 2 * rows, taps), jnp.bfloat16),
        ),
        in_specs=[pl.BlockSpec(memory_space=pl.ANY), vmem, pl.BlockSpec(memory_space=pl.ANY)],
        out_specs=(vmem, vmem),
        scratch_shapes=[
            pltpu.VMEM(template_bank.shape, jnp.bfloat16),
            pltpu.SemaphoreType.DMA,
            pltpu.SemaphoreType.DMA((send_count,)),
            pltpu.SemaphoreType.DMA((plan.slot_count,)),
        ],
        compiler_params=pltpu.CompilerParams(
            collective_id=0, has_side_effects=True, vmem_limit_bytes=16 << 20
        ),
        name="gather",
    )(spectrum, template_index.reshape(1, rows), template_bank)
    return pl.pallas_call(
        functools.partial(search_kernel, plan),
        out_shape=jax.ShapeDtypeStruct((rows, cols), jnp.float32),
        in_specs=[vmem, vmem],
        out_specs=vmem,
        scratch_shapes=[
            pltpu.VMEM((plan.width, CHUNK), jnp.bfloat16),
            pltpu.VMEM((plan.width, CHUNK), jnp.bfloat16),
            pltpu.VMEM((rows, plan.part_cols[1]), jnp.bfloat16),
            pltpu.VMEM((rows, plan.part_cols[2]), jnp.bfloat16),
            pltpu.VMEM((rows, plan.part_cols[3]), jnp.bfloat16),
        ],
        compiler_params=pltpu.CompilerParams(vmem_limit_bytes=32 << 20),
        name="search",
    )(windows, lhs)


def solution(mesh):
    return jax.shard_map(
        body,
        mesh=mesh,
        in_specs=(P(None, ("beam", "freq")), P(), P()),
        out_specs=P(None, ("beam", "freq")),
        check_vma=False,
    )
```

```python
import functools

import jax
import jax.numpy as jnp
from jax import lax
from jax.experimental import pallas as pl
from jax.experimental.pallas import tpu as pltpu
from jax.sharding import PartitionSpec as P

RATIOS = ((1, 1), (1, 2), (1, 4), (3, 4))
CHUNK = 256
LANES = 128


class Plan:
    def __init__(self, cols, taps, rows, owners):
        self.cols, self.taps, self.rows, self.owners = cols, taps, rows, owners
        self.granule = taps // 2
        self.held = cols // self.granule
        self.steps = [self.held * n // d for n, d in RATIOS]
        self.part_cols = [cols * n // d for n, d in RATIOS]
        self.part_rows = [rows * n // d for n, d in RATIOS]
        self.offsets, self.slots = [], []
        offset = slot = 0
        for width in self.part_cols:
            self.offsets.append(offset)
            self.slots.append(slot)
            offset += width + taps
            slot += (width + taps) // self.granule
        self.width, self.slot_count = offset, slot


def sends(plan, me):
    found = []
    for own in range(plan.held):
        for part, step in enumerate(plan.steps):
            spot = plan.held * me + own + 1
            last = spot // step
            rest = spot - last * step
            for back in range((step + 1) // step + 1):
                if plan.held % step == 0:
                    if (own + 1) % step + step * back >= step + 2:
                        continue
                to = last - back
                place = rest + step * back
                fits = (to >= 0) & (to < plan.owners) & (place < step + 2)
                found.append((own, part, to, place, fits))
    return found


def gather_kernel(plan, spec_ref, index_ref, bank_ref, win_ref, lhs_ref, bank, index, bank_sem, index_sem, send_sems, recv_sems):
    me = lax.axis_index("freq")
    size = plan.granule
    rows = plan.rows
    fetch = pltpu.make_async_copy(bank_ref, bank, bank_sem)
    fetch.start()
    fetch_index = pltpu.make_async_copy(index_ref, index, index_sem)
    fetch_index.start()
    barrier = pltpu.get_barrier_semaphore()

    def greet(step, carry):
        peer = lax.rem(me + step, plan.owners)
        pl.semaphore_signal(barrier, inc=1, device_id={"freq": peer}, device_id_type=pl.DeviceIdType.MESH)
        return carry

    lax.fori_loop(1, plan.owners, greet, 0)

    @pl.when(me == 0)
    def _():
        for offset in plan.offsets:
            win_ref[:, offset : offset + size] = jnp.zeros((2, size), win_ref.dtype)

    @pl.when(me == plan.owners - 1)
    def _():
        end = plan.offsets[0] + plan.part_cols[0] + plan.taps
        win_ref[:, end - size : end] = jnp.zeros((2, size), win_ref.dtype)

    pl.semaphore_wait(barrier, plan.owners - 1)

    def each(act_remote, act_local):
        for number, (own, part, to, place, fits) in enumerate(sends(plan, me)):
            source = spec_ref.at[:, own * size : (own + 1) * size]
            target = win_ref.at[:, pl.ds(pl.multiple_of(plan.offsets[part] + place * size, size), size)]
            got = recv_sems.at[plan.slots[part] + place]

            @pl.when(fits & (to != me))
            def _():
                act_remote(
                    pltpu.make_async_remote_copy(
                        src_ref=source,
                        dst_ref=target,
                        send_sem=send_sems.at[number],
                        recv_sem=got,
                        device_id={"freq": to},
                        device_id_type=pl.DeviceIdType.MESH,
                    )
                )

            if act_local is not None:

                @pl.when(fits & (to == me))
                def _():
                    act_local(pltpu.make_async_copy(source, target, got))

    each(lambda copy: copy.start(), lambda copy: copy.start())

    fetch_index.wait()
    fetch.wait()
    names = lax.broadcasted_iota(jnp.int32, (bank.shape[1], rows), 0)
    picks = (names == index[...]).astype(jnp.float32).T.astype(jnp.bfloat16)
    real = jnp.dot(picks, bank[0], preferred_element_type=jnp.float32).astype(jnp.bfloat16)
    imag = jnp.dot(picks, bank[1], preferred_element_type=jnp.float32).astype(jnp.bfloat16)
    lhs_ref[0, :rows] = real
    lhs_ref[0, rows:] = imag
    lhs_ref[1, :rows] = -imag
    lhs_ref[1, rows:] = real

    for part, step in enumerate(plan.steps):
        for place in range(step + 2):
            spot = step * me - 1 + place

            @pl.when((spot >= 0) & (spot < plan.held * plan.owners))
            def _():
                start = plan.offsets[part] + place * size
                pltpu.make_async_copy(
                    spec_ref.at[:, 0:size],
                    win_ref.at[:, start : start + size],
                    recv_sems.at[plan.slots[part] + place],
                ).wait()

    each(lambda copy: copy.wait_send(), None)


def one_hot(shape, make):
    left = lax.broadcasted_iota(jnp.int32, shape, 0)
    right = lax.broadcasted_iota(jnp.int32, shape, 1)
    return make(left, right).astype(jnp.float32).astype(jnp.bfloat16)


def search_kernel(plan, win_ref, lhs_ref, out_ref, *scratch):
    rows, taps = plan.rows, plan.taps
    parts = len(RATIOS)
    shifts, held = scratch[: 2 * parts], scratch[2 * parts :]

    def build(part):
        width = plan.part_cols[part] + taps
        start = plan.offsets[part]
        bases = []

        def first(which):
            line = win_ref[which : which + 1, start : start + width].astype(jnp.float32)
            base = jnp.broadcast_to(line, (8, width))
            place = lax.broadcasted_iota(jnp.int32, (8, width), 0)
            for bit in (1, 2, 4):
                base = jnp.where((place & bit) != 0, pltpu.roll(base, width - bit, 1), base)
            base = jnp.concatenate([base, pltpu.roll(base, width - 8, 1)], 0)
            bases.append(base.astype(jnp.bfloat16))

        def turned(which, turn):
            base = bases[which]
            into = shifts[2 * part + which]
            moved = base if turn == 0 else pltpu.roll(base, width - 16 * turn, 1)
            for block in range(width // LANES):
                piece = moved[:, block * LANES : (block + 1) * LANES]
                spot = block * LANES + 16 * turn
                into[spot : spot + 16, 0:LANES] = piece
                if block:
                    into[spot - LANES : spot - LANES + 16, LANES : 2 * LANES] = piece

        tasks = [functools.partial(first, which) for which in (0, 1)]
        tasks += [functools.partial(turned, which, turn) for turn in range(LANES // 16) for which in (0, 1)]
        return tasks

    def power(part, chunk):
        count = plan.part_rows[part]
        start = chunk * CHUNK

        def left(which):
            if count == rows:
                return lhs_ref[which]
            return jnp.concatenate([lhs_ref[which, :count], lhs_ref[which, rows : rows + count]], 0)

        both = sum(
            jnp.dot(left(which), shifts[2 * part + which][start : start + taps, :], preferred_element_type=jnp.float32)
            for which in (0, 1)
        )
        real, imag = both[:count], both[count:]
        return (real * real + imag * imag).astype(jnp.bfloat16)

    def fill(part, chunk):
        n, d = RATIOS[part]
        spread = one_hot((rows, plan.part_rows[part]), lambda z, k: z * n // d == k)
        cells = jnp.dot(spread, power(part, chunk), preferred_element_type=jnp.float32)
        held[part - 1][:, chunk * CHUNK : (chunk + 1) * CHUNK] = cells.astype(jnp.bfloat16)

    half = one_hot((LANES, CHUNK), lambda k, r: k == r // 2)
    quarters = [one_hot((LANES, CHUNK), lambda k, r: k == CHUNK // 4 * odd + r // 4) for odd in (0, 1)]
    threes = [one_hot((CHUNK, CHUNK), lambda k, r: k == CHUNK // 4 * odd + 3 * r // 4) for odd in (0, 1)]

    def finish(chunk):
        step, odd = divmod(chunk, 2)
        total = power(0, chunk).astype(jnp.float32)
        spots = (
            (held[0], chunk * LANES, half),
            (held[1], step * LANES, quarters[odd]),
            (held[2], (3 * step + odd) * LANES, threes[odd]),
        )
        cells = jnp.concatenate([ref[:, at : at + spread.shape[0]] for ref, at, spread in spots], 1)
        spreads = jnp.concatenate([spread for _, _, spread in spots], 0)
        total += jnp.dot(cells, spreads, preferred_element_type=jnp.float32)
        out_ref[:, chunk * CHUNK : (chunk + 1) * CHUNK] = total

    def run(products, builds):
        done = 0
        for number, product in enumerate(products):
            product()
            until = len(builds) * (number + 1) // len(products)
            for task in builds[done:until]:
                task()
            done = until

    def fills(part):
        return [functools.partial(fill, part, chunk) for chunk in range(plan.part_cols[part] // CHUNK)]

    for task in build(2):
        task()
    run(fills(2), build(1))
    run(fills(1), build(3))
    run(fills(3), build(0))
    run([functools.partial(finish, chunk) for chunk in range(plan.cols // CHUNK)], [])


def body(spectrum, template_bank, template_index):
    owners = lax.axis_size("freq")
    bank_count, taps = template_bank.shape[1:]
    rows = template_index.shape[0]
    cols = spectrum.shape[1]
    plan = Plan(cols, taps, rows, owners)
    send_count = len(sends(plan, 0))
    vmem = pl.BlockSpec(memory_space=pltpu.VMEM)
    windows, lhs = pl.pallas_call(
        functools.partial(gather_kernel, plan),
        out_shape=(
            jax.ShapeDtypeStruct((2, plan.width), jnp.bfloat16),
            jax.ShapeDtypeStruct((2, 2 * rows, taps), jnp.bfloat16),
        ),
        in_specs=[pl.BlockSpec(memory_space=pltpu.HBM)] * 3,
        out_specs=(vmem, vmem),
        scratch_shapes=[
            pltpu.VMEM(template_bank.shape, jnp.bfloat16),
            pltpu.VMEM((1, rows), jnp.int32),
            pltpu.SemaphoreType.DMA,
            pltpu.SemaphoreType.DMA,
            pltpu.SemaphoreType.DMA((send_count,)),
            pltpu.SemaphoreType.DMA((plan.slot_count,)),
        ],
        compiler_params=pltpu.CompilerParams(
            collective_id=0, has_side_effects=True, vmem_limit_bytes=16 << 20
        ),
        name="gather",
    )(spectrum, template_index.reshape(1, rows), template_bank)
    return pl.pallas_call(
        functools.partial(search_kernel, plan),
        out_shape=jax.ShapeDtypeStruct((rows, cols), jnp.float32),
        in_specs=[vmem, vmem],
        out_specs=vmem,
        scratch_shapes=[
            *[pltpu.VMEM((width + taps, CHUNK), jnp.bfloat16) for width in plan.part_cols for _ in range(2)],
            *[pltpu.VMEM((rows, width), jnp.bfloat16) for width in plan.part_cols[1:]],
        ],
        compiler_params=pltpu.CompilerParams(vmem_limit_bytes=32 << 20),
        name="search",
    )(windows, lhs)


def solution(mesh):
    return jax.shard_map(
        body,
        mesh=mesh,
        in_specs=(P(None, ("beam", "freq")), P(), P()),
        out_specs=P(None, ("beam", "freq")),
        check_vma=False,
    )
```

```python
import functools

import jax
import jax.numpy as jnp
from jax import lax
from jax.experimental import pallas as pl
from jax.experimental.pallas import tpu as pltpu
from jax.sharding import PartitionSpec as P

RATIOS = ((1, 1), (1, 2), (1, 4), (3, 4))
CHUNK = 256
LANES = 128


class Plan:
    def __init__(self, cols, taps, rows, owners):
        self.cols, self.taps, self.rows, self.owners = cols, taps, rows, owners
        self.granule = taps // 2
        self.held = cols // self.granule
        self.steps = [self.held * n // d for n, d in RATIOS]
        self.part_cols = [cols * n // d for n, d in RATIOS]
        self.part_rows = [rows * n // d for n, d in RATIOS]
        self.offsets, self.slots = [], []
        offset = slot = 0
        for width in self.part_cols:
            self.offsets.append(offset)
            self.slots.append(slot)
            offset += width + taps
            slot += (width + taps) // self.granule
        self.width, self.slot_count = offset, slot


def sends(plan, me):
    found = []
    for own in range(plan.held):
        for part, step in enumerate(plan.steps):
            spot = plan.held * me + own + 1
            last = spot // step
            rest = spot - last * step
            for back in range((step + 1) // step + 1):
                if plan.held % step == 0:
                    if (own + 1) % step + step * back >= step + 2:
                        continue
                to = last - back
                place = rest + step * back
                fits = (to >= 0) & (to < plan.owners) & (place < step + 2)
                found.append((own, part, to, place, fits))
    return found


def one_hot(shape, make):
    left = lax.broadcasted_iota(jnp.int32, shape, 0)
    right = lax.broadcasted_iota(jnp.int32, shape, 1)
    return make(left, right).astype(jnp.float32).astype(jnp.bfloat16)


def search_kernel(plan, spec_ref, index_ref, bank_ref, out_ref, win, bank, index, lhs, plane, *scratch):
    rows, taps, size = plan.rows, plan.taps, plan.granule
    parts = len(RATIOS)
    shifts, held = scratch[: 2 * parts], scratch[2 * parts : 3 * parts - 1]
    bank_sem, index_sem, own_sem, send_sems, recv_sems = scratch[3 * parts - 1 :]
    me = lax.axis_index("freq")

    own_start = plan.offsets[0] + size
    fetch_own = pltpu.make_async_copy(spec_ref, win.at[:, own_start : own_start + plan.cols], own_sem)
    fetch_own.start()
    fetch_index = pltpu.make_async_copy(index_ref, index, index_sem)
    fetch_index.start()
    fetch_bank = pltpu.make_async_copy(bank_ref, bank, bank_sem)
    fetch_bank.start()

    barrier = pltpu.get_barrier_semaphore()

    def greet(step, carry):
        peer = lax.rem(me + step, plan.owners)
        pl.semaphore_signal(barrier, inc=1, device_id={"freq": peer}, device_id_type=pl.DeviceIdType.MESH)
        return carry

    lax.fori_loop(1, plan.owners, greet, 0)

    @pl.when(me == 0)
    def _():
        for offset in plan.offsets:
            win[:, offset : offset + size] = jnp.zeros((2, size), win.dtype)

    @pl.when(me == plan.owners - 1)
    def _():
        end = plan.offsets[0] + plan.part_cols[0] + plan.taps
        win[:, end - size : end] = jnp.zeros((2, size), win.dtype)

    def each(act_remote, act_local):
        for number, (own, part, to, place, fits) in enumerate(sends(plan, me)):
            source = spec_ref.at[:, own * size : (own + 1) * size]
            target = win.at[:, pl.ds(pl.multiple_of(plan.offsets[part] + place * size, size), size)]
            got = recv_sems.at[plan.slots[part] + place]

            @pl.when(fits & (to != me))
            def _():
                act_remote(
                    pltpu.make_async_remote_copy(
                        src_ref=source,
                        dst_ref=target,
                        send_sem=send_sems.at[number],
                        recv_sem=got,
                        device_id={"freq": to},
                        device_id_type=pl.DeviceIdType.MESH,
                    )
                )

            if act_local is not None and part:

                @pl.when(fits & (to == me))
                def _():
                    act_local(pltpu.make_async_copy(source, target, got))

    def receive(part):
        step = plan.steps[part]
        for place in range(step + 2):
            if part == 0 and 0 < place <= plan.held:
                continue
            spot = step * me - 1 + place

            @pl.when((spot >= 0) & (spot < plan.held * plan.owners))
            def _():
                start = plan.offsets[part] + place * size
                pltpu.make_async_copy(
                    spec_ref.at[:, 0:size],
                    win.at[:, start : start + size],
                    recv_sems.at[plan.slots[part] + place],
                ).wait()

    def build(part, low, high):
        width = (high - low + 1) * LANES
        start = plan.offsets[part] + low * LANES
        bases = []

        def first(which):
            line = win[which : which + 1, start : start + width].astype(jnp.float32)
            base = jnp.broadcast_to(line, (8, width))
            place = lax.broadcasted_iota(jnp.int32, (8, width), 0)
            for bit in (1, 2, 4):
                base = jnp.where((place & bit) != 0, pltpu.roll(base, width - bit, 1), base)
            base = jnp.concatenate([base, pltpu.roll(base, width - 8, 1)], 0)
            bases.append(base.astype(jnp.bfloat16))

        def turned(which, turn):
            base = bases[which]
            into = shifts[2 * part + which]
            moved = base if turn == 0 else pltpu.roll(base, width - 16 * turn, 1)
            for block in range(high - low):
                piece = moved[:, block * LANES : (block + 1) * LANES]
                spot = (low + block) * LANES + 16 * turn
                into[spot : spot + 16, 0:LANES] = piece
                if spot >= LANES:
                    into[spot - LANES : spot - LANES + 16, LANES : 2 * LANES] = piece

        tasks = [functools.partial(first, which) for which in (0, 1)]
        tasks += [functools.partial(turned, which, turn) for turn in range(LANES // 16) for which in (0, 1)]
        return tasks

    def power(part, chunk):
        count = plan.part_rows[part]
        start = chunk * CHUNK
        if count == rows:
            left = lhs[...]
        else:
            left = jnp.concatenate([lhs[:count], lhs[rows : rows + count]], 0)
        right = jnp.concatenate([shifts[2 * part + which][start : start + taps, :] for which in (0, 1)], 0)
        both = jnp.dot(left, right, preferred_element_type=jnp.float32)
        real, imag = both[:count], both[count:]
        return (real * real + imag * imag).astype(jnp.bfloat16)

    def keep(chunk):
        plane[:, chunk * CHUNK : (chunk + 1) * CHUNK] = power(0, chunk)

    def fill(part, chunk):
        n, d = RATIOS[part]
        spread = one_hot((rows, plan.part_rows[part]), lambda z, k: z * n // d == k)
        cells = jnp.dot(spread, power(part, chunk), preferred_element_type=jnp.float32)
        held[part - 1][:, chunk * CHUNK : (chunk + 1) * CHUNK] = cells.astype(jnp.bfloat16)

    def finish(chunk):
        half = one_hot((LANES, CHUNK), lambda k, r: k == r // 2)
        quarters = [one_hot((LANES, CHUNK), lambda k, r: k == CHUNK // 4 * odd + r // 4) for odd in (0, 1)]
        threes = [one_hot((CHUNK, CHUNK), lambda k, r: k == CHUNK // 4 * odd + 3 * r // 4) for odd in (0, 1)]
        step, odd = divmod(chunk, 2)
        spots = (
            (held[0], chunk * LANES, half),
            (held[1], step * LANES, quarters[odd]),
            (held[2], (3 * step + odd) * LANES, threes[odd]),
        )
        cells = jnp.concatenate([ref[:, at : at + spread.shape[0]] for ref, at, spread in spots], 1)
        spreads = jnp.concatenate([spread for _, _, spread in spots], 0)
        total = plane[:, chunk * CHUNK : (chunk + 1) * CHUNK].astype(jnp.float32)
        total += jnp.dot(cells, spreads, preferred_element_type=jnp.float32)
        out_ref[:, chunk * CHUNK : (chunk + 1) * CHUNK] = total

    def run(products, builds):
        done = 0
        for number, product in enumerate(products):
            product()
            until = len(builds) * (number + 1) // len(products)
            for task in builds[done:until]:
                task()
            done = until

    def fills(part):
        return [functools.partial(fill, part, chunk) for chunk in range(plan.part_cols[part] // CHUNK)]

    def whole(part):
        return build(part, 0, (plan.part_cols[part] + taps) // LANES - 1)

    halo = size // LANES
    last = (plan.cols + taps) // LANES - 1

    fetch_own.wait()
    for task in build(0, halo, last - halo):
        task()
    pl.semaphore_wait(barrier, plan.owners - 1)
    each(lambda copy: copy.start(), lambda copy: copy.start())

    fetch_index.wait()
    fetch_bank.wait()
    names = lax.broadcasted_iota(jnp.int32, (bank.shape[1], rows), 0)
    picks = (names == index[...]).astype(jnp.float32).T.astype(jnp.bfloat16)
    real = jnp.dot(picks, bank[0], preferred_element_type=jnp.float32).astype(jnp.bfloat16)
    imag = jnp.dot(picks, bank[1], preferred_element_type=jnp.float32).astype(jnp.bfloat16)
    lhs[:rows, :taps] = real
    lhs[rows:, :taps] = imag
    lhs[:rows, taps:] = -imag
    lhs[rows:, taps:] = real

    chunks = plan.cols // CHUNK
    edge = size // CHUNK
    for chunk in range(edge, chunks - edge):
        keep(chunk)
    receive(0)
    for task in build(0, 0, halo) + build(0, last - halo, last):
        task()
    for chunk in [*range(edge), *range(chunks - edge, chunks)]:
        keep(chunk)
    for part in range(1, parts):
        receive(part)
    for task in whole(2):
        task()
    run(fills(2), whole(1))
    run(fills(1), whole(3))
    run(fills(3), [])
    for chunk in range(chunks):
        finish(chunk)

    each(lambda copy: copy.wait_send(), None)


def body(spectrum, template_bank, template_index):
    owners = lax.axis_size("freq")
    taps = template_bank.shape[2]
    rows = template_index.shape[0]
    cols = spectrum.shape[1]
    plan = Plan(cols, taps, rows, owners)
    send_count = len(sends(plan, 0))
    return pl.pallas_call(
        functools.partial(search_kernel, plan),
        out_shape=jax.ShapeDtypeStruct((rows, cols), jnp.float32),
        in_specs=[pl.BlockSpec(memory_space=pl.ANY)] * 3,
        out_specs=pl.BlockSpec(memory_space=pltpu.VMEM),
        scratch_shapes=[
            pltpu.VMEM((2, plan.width), jnp.bfloat16),
            pltpu.VMEM(template_bank.shape, jnp.bfloat16),
            pltpu.VMEM((1, rows), jnp.int32),
            pltpu.VMEM((2 * rows, 2 * taps), jnp.bfloat16),
            pltpu.VMEM((rows, cols), jnp.bfloat16),
            *[pltpu.VMEM((width + taps, CHUNK), jnp.bfloat16) for width in plan.part_cols for _ in range(2)],
            *[pltpu.VMEM((rows, width), jnp.bfloat16) for width in plan.part_cols[1:]],
            pltpu.SemaphoreType.DMA,
            pltpu.SemaphoreType.DMA,
            pltpu.SemaphoreType.DMA,
            pltpu.SemaphoreType.DMA((send_count,)),
            pltpu.SemaphoreType.DMA((plan.slot_count,)),
        ],
        compiler_params=pltpu.CompilerParams(collective_id=0, has_side_effects=True),
        name="search",
    )(spectrum, template_index.reshape(1, rows), template_bank)


def solution(mesh):
    return jax.shard_map(
        body,
        mesh=mesh,
        in_specs=(P(None, ("beam", "freq")), P(), P()),
        out_specs=P(None, ("beam", "freq")),
        check_vma=False,
    )
```

```python
import functools

import jax
import jax.numpy as jnp
from jax import lax
from jax.experimental import pallas as pl
from jax.experimental.pallas import tpu as pltpu
from jax.sharding import PartitionSpec as P

RATIOS = ((1, 1), (1, 2), (1, 4), (3, 4))
CHUNK = 256
LANES = 128


class Plan:
    def __init__(self, cols, taps, rows, owners):
        self.cols, self.taps, self.rows, self.owners = cols, taps, rows, owners
        self.granule = taps // 2
        self.held = cols // self.granule
        self.steps = [self.held * n // d for n, d in RATIOS]
        self.part_cols = [cols * n // d for n, d in RATIOS]
        self.part_rows = [rows * n // d for n, d in RATIOS]
        self.offsets, self.slots = [], []
        offset = slot = 0
        for width in self.part_cols:
            self.offsets.append(offset)
            self.slots.append(slot)
            offset += width + taps if self.offsets[1:] else 0
            slot += (width + taps) // self.granule
        self.width, self.slot_count = offset, slot


def sends(plan, me):
    found = []
    for own in range(plan.held):
        for part, step in enumerate(plan.steps):
            spot = plan.held * me + own + 1
            last = spot // step
            rest = spot - last * step
            for back in range((step + 1) // step + 1):
                if plan.held % step == 0:
                    if (own + 1) % step + step * back >= step + 2:
                        continue
                to = last - back
                place = rest + step * back
                fits = (to >= 0) & (to < plan.owners) & (place < step + 2)
                found.append((own, part, to, place, fits))
    return found


def one_hot(shape, make):
    left = lax.broadcasted_iota(jnp.int32, shape, 0)
    right = lax.broadcasted_iota(jnp.int32, shape, 1)
    return make(left, right).astype(jnp.float32).astype(jnp.bfloat16)


def build(window, shifts, low, high):
    width = (high - low + 1) * LANES
    start = low * LANES
    bases = []

    def first(which):
        line = window[which : which + 1, start : start + width].astype(jnp.float32)
        base = jnp.broadcast_to(line, (8, width))
        place = lax.broadcasted_iota(jnp.int32, (8, width), 0)
        for bit in (1, 2, 4):
            base = jnp.where((place & bit) != 0, pltpu.roll(base, width - bit, 1), base)
        base = jnp.concatenate([base, pltpu.roll(base, width - 8, 1)], 0)
        bases.append(base.astype(jnp.bfloat16))

    def turned(which, turn):
        base = bases[which]
        into = shifts[which]
        moved = base if turn == 0 else pltpu.roll(base, width - 16 * turn, 1)
        for block in range(high - low):
            piece = moved[:, block * LANES : (block + 1) * LANES]
            spot = (low + block) * LANES + 16 * turn
            into[spot : spot + 16, 0:LANES] = piece
            if spot >= LANES:
                into[spot - LANES : spot - LANES + 16, LANES : 2 * LANES] = piece

    tasks = [functools.partial(first, which) for which in (0, 1)]
    tasks += [functools.partial(turned, which, turn) for turn in range(LANES // 16) for which in (0, 1)]
    return tasks


def power(lhs, shifts, count, taps, start, width):
    rows = lhs.shape[0] // 2
    if count == rows:
        left = lhs[...]
    else:
        left = jnp.concatenate([lhs[:count], lhs[rows : rows + count]], 0)
    right = jnp.concatenate(
        [
            jnp.concatenate(
                [shifts[which][start + at : start + at + taps, :] for at in range(0, width, CHUNK)], 1
            )
            for which in (0, 1)
        ],
        0,
    )
    both = jnp.dot(left, right, preferred_element_type=jnp.float32)
    real, imag = both[:count], both[count:]
    return (real * real + imag * imag).astype(jnp.bfloat16)


def gather_kernel(plan, spec_ref, index_ref, bank_ref, win_out, lhs_out, plane_out, win, bank, index, lhs, plane, *scratch):
    rows, taps, size = plan.rows, plan.taps, plan.granule
    parts = len(RATIOS)
    shifts = scratch[:2]
    bank_sem, index_sem, own_sem, out_sems, send_sems, recv_sems = scratch[2:]
    me = lax.axis_index("freq")

    own_start = size
    fetch_own = pltpu.make_async_copy(spec_ref, win.at[:, own_start : own_start + plan.cols], own_sem)
    fetch_own.start()
    fetch_index = pltpu.make_async_copy(index_ref, index, index_sem)
    fetch_index.start()
    fetch_bank = pltpu.make_async_copy(bank_ref, bank, bank_sem)
    fetch_bank.start()

    barrier = pltpu.get_barrier_semaphore()

    def greet(step, carry):
        peer = lax.rem(me + step, plan.owners)
        pl.semaphore_signal(barrier, inc=1, device_id={"freq": peer}, device_id_type=pl.DeviceIdType.MESH)
        return carry

    lax.fori_loop(1, plan.owners, greet, 0)

    @pl.when(me == 0)
    def _():
        win[:, 0:size] = jnp.zeros((2, size), win.dtype)

    @pl.when(me == plan.owners - 1)
    def _():
        end = plan.cols + plan.taps
        win[:, end - size : end] = jnp.zeros((2, size), win.dtype)

    def each(act_remote, act_local):
        for number, (own, part, to, place, fits) in enumerate(sends(plan, me)):
            source = spec_ref.at[:, own * size : (own + 1) * size]
            into = win if part == 0 else win_out
            target = into.at[:, pl.ds(pl.multiple_of(plan.offsets[part] + place * size, size), size)]
            got = recv_sems.at[plan.slots[part] + place]

            @pl.when(fits & (to != me))
            def _():
                act_remote(
                    pltpu.make_async_remote_copy(
                        src_ref=source,
                        dst_ref=target,
                        send_sem=send_sems.at[number],
                        recv_sem=got,
                        device_id={"freq": to},
                        device_id_type=pl.DeviceIdType.MESH,
                    )
                )

            if act_local is not None and part:

                @pl.when(fits & (to == me))
                def _():
                    act_local(pltpu.make_async_copy(source, target, got))

    def receive(part):
        step = plan.steps[part]
        for place in range(step + 2):
            if part == 0 and 0 < place <= plan.held:
                continue
            spot = step * me - 1 + place

            def land():
                start = plan.offsets[part] + place * size
                pltpu.make_async_copy(
                    spec_ref.at[:, 0:size],
                    (win if part == 0 else win_out).at[:, start : start + size],
                    recv_sems.at[plan.slots[part] + place],
                ).wait()

            if part:
                land()
            else:
                pl.when((spot >= 0) & (spot < plan.held * plan.owners))(land)

    def keep(chunk):
        plane[:, chunk * CHUNK : (chunk + 1) * CHUNK] = power(lhs, shifts, rows, taps, chunk * CHUNK, CHUNK)

    halo = size // LANES
    last = (plan.cols + taps) // LANES - 1

    fetch_own.wait()
    for task in build(win, shifts, halo, last - halo):
        task()
    pl.semaphore_wait(barrier, plan.owners - 1)
    each(lambda copy: copy.start(), lambda copy: copy.start())

    @pl.when(me == 0)
    def _():
        for part in range(1, parts):
            start = plan.offsets[part]
            pltpu.make_async_copy(
                win.at[:, 0:size], win_out.at[:, start : start + size], recv_sems.at[plan.slots[part]]
            ).start()

    fetch_index.wait()
    fetch_bank.wait()
    names = lax.broadcasted_iota(jnp.int32, (bank.shape[1], rows), 0)
    picks = (names == index[...]).astype(jnp.float32).T.astype(jnp.bfloat16)
    real = jnp.dot(picks, bank[0], preferred_element_type=jnp.float32).astype(jnp.bfloat16)
    imag = jnp.dot(picks, bank[1], preferred_element_type=jnp.float32).astype(jnp.bfloat16)
    lhs[:rows, :taps] = real
    lhs[rows:, :taps] = imag
    lhs[:rows, taps:] = -imag
    lhs[rows:, taps:] = real

    chunks = plan.cols // CHUNK
    edge = size // CHUNK
    for chunk in range(edge, chunks - edge):
        keep(chunk)
    put_lhs = pltpu.make_async_copy(lhs, lhs_out, out_sems.at[0])
    put_lhs.start()
    receive(0)
    for task in build(win, shifts, 0, halo) + build(win, shifts, last - halo, last):
        task()
    for chunk in [*range(edge), *range(chunks - edge, chunks)]:
        keep(chunk)
    put_plane = pltpu.make_async_copy(plane, plane_out, out_sems.at[1])
    put_plane.start()
    for part in range(1, parts):
        receive(part)
    put_lhs.wait()
    put_plane.wait()
    each(lambda copy: copy.wait_send(), None)


def search_kernel(plan, win_ref, lhs_ref, plane_ref, out_ref, win, lhs, plane, out, *scratch):
    rows, taps = plan.rows, plan.taps
    parts = len(RATIOS)
    shifts, held = scratch[: 2 * parts - 2], scratch[2 * parts - 2 : 3 * parts - 3]
    in_sems, out_sems = scratch[3 * parts - 3 :]
    offsets = plan.offsets
    fetch_win = pltpu.make_async_copy(win_ref, win, in_sems.at[0])
    fetch_lhs = pltpu.make_async_copy(lhs_ref, lhs, in_sems.at[1])
    fetch_plane = pltpu.make_async_copy(plane_ref, plane, in_sems.at[2])
    fetch_win.start()
    fetch_lhs.start()
    fetch_plane.start()

    def put(chunk):
        spot = slice(chunk * CHUNK, (chunk + 1) * CHUNK)
        return pltpu.make_async_copy(out.at[:, spot], out_ref.at[:, spot], out_sems.at[chunk])

    def fill(part, start):
        width = 2 * CHUNK
        n, d = RATIOS[part]
        spread = one_hot((rows, plan.part_rows[part]), lambda z, k: z * n // d == k)
        cells = jnp.dot(spread, power(lhs, shifts[2 * part - 2 : 2 * part], plan.part_rows[part], taps, start, width), preferred_element_type=jnp.float32)
        held[part - 1][:, start : start + width] = cells.astype(jnp.bfloat16)

    def finish(chunk):
        half = one_hot((LANES, CHUNK), lambda k, r: k == r // 2)
        quarters = [one_hot((LANES, CHUNK), lambda k, r: k == CHUNK // 4 * odd + r // 4) for odd in (0, 1)]
        threes = [one_hot((CHUNK, CHUNK), lambda k, r: k == CHUNK // 4 * odd + 3 * r // 4) for odd in (0, 1)]
        step, odd = divmod(chunk, 2)
        spots = (
            (held[0], chunk * LANES, half),
            (held[1], step * LANES, quarters[odd]),
            (held[2], (3 * step + odd) * LANES, threes[odd]),
        )
        cells = jnp.concatenate([ref[:, at : at + spread.shape[0]] for ref, at, spread in spots], 1)
        spreads = jnp.concatenate([spread for _, _, spread in spots], 0)
        total = plane[:, chunk * CHUNK : (chunk + 1) * CHUNK].astype(jnp.float32)
        total += jnp.dot(cells, spreads, preferred_element_type=jnp.float32)
        out[:, chunk * CHUNK : (chunk + 1) * CHUNK] = total
        put(chunk).start()

    def run(products, builds):
        done = 0
        for number, product in enumerate(products):
            product()
            until = len(builds) * (number + 1) // len(products)
            for task in builds[done:until]:
                task()
            done = until

    def fills(part):
        return [functools.partial(fill, part, start) for start in range(0, plan.part_cols[part], 2 * CHUNK)]

    def whole(part):
        return build(win.at[:, offsets[part] : offsets[part] + plan.part_cols[part] + taps], shifts[2 * part - 2 : 2 * part], 0, (plan.part_cols[part] + taps) // LANES - 1)

    fetch_win.wait()
    for task in whole(2):
        task()
    fetch_lhs.wait()
    run(fills(2), whole(1))
    run(fills(1), whole(3))
    run(fills(3), [])
    fetch_plane.wait()
    for chunk in range(plan.cols // CHUNK):
        finish(chunk)
    for chunk in range(plan.cols // CHUNK):
        put(chunk).wait()


def body(spectrum, template_bank, template_index):
    owners = lax.axis_size("freq")
    taps = template_bank.shape[2]
    rows = template_index.shape[0]
    cols = spectrum.shape[1]
    plan = Plan(cols, taps, rows, owners)
    hbm = pl.BlockSpec(memory_space=pl.ANY)
    between = (
        ((2, plan.width), jnp.bfloat16),
        ((2 * rows, 2 * taps), jnp.bfloat16),
        ((rows, cols), jnp.bfloat16),
    )
    windows, lhs, plane = pl.pallas_call(
        functools.partial(gather_kernel, plan),
        out_shape=tuple(jax.ShapeDtypeStruct(*item) for item in between),
        in_specs=[hbm] * 3,
        out_specs=(hbm,) * 3,
        scratch_shapes=[
            pltpu.VMEM((2, cols + taps), jnp.bfloat16),
            pltpu.VMEM(template_bank.shape, jnp.bfloat16),
            pltpu.VMEM((1, rows), jnp.int32),
            *[pltpu.VMEM(*item) for item in between[1:]],
            *[pltpu.VMEM((cols + taps, CHUNK), jnp.bfloat16) for _ in range(2)],
            pltpu.SemaphoreType.DMA,
            pltpu.SemaphoreType.DMA,
            pltpu.SemaphoreType.DMA,
            pltpu.SemaphoreType.DMA((2,)),
            pltpu.SemaphoreType.DMA((len(sends(plan, 0)),)),
            pltpu.SemaphoreType.DMA((plan.slot_count,)),
        ],
        compiler_params=pltpu.CompilerParams(collective_id=0, has_side_effects=True),
        name="gather",
    )(spectrum, template_index.reshape(1, rows), template_bank)
    return pl.pallas_call(
        functools.partial(search_kernel, plan),
        out_shape=jax.ShapeDtypeStruct((rows, cols), jnp.float32),
        in_specs=[hbm] * 3,
        out_specs=hbm,
        scratch_shapes=[
            *[pltpu.VMEM(*item) for item in between],
            pltpu.VMEM((rows, cols), jnp.float32),
            *[pltpu.VMEM((width + taps, CHUNK), jnp.bfloat16) for width in plan.part_cols[1:] for _ in range(2)],
            *[pltpu.VMEM((rows, width), jnp.bfloat16) for width in plan.part_cols[1:]],
            pltpu.SemaphoreType.DMA((3,)),
            pltpu.SemaphoreType.DMA((cols // CHUNK,)),
        ],
        name="search",
    )(windows, lhs, plane)


def solution(mesh):
    return jax.shard_map(
        body,
        mesh=mesh,
        in_specs=(P(None, ("beam", "freq")), P(), P()),
        out_specs=P(None, ("beam", "freq")),
        check_vma=False,
    )
```

```python
import functools

import jax
import jax.numpy as jnp
from jax import lax
from jax.experimental import pallas as pl
from jax.experimental.pallas import tpu as pltpu
from jax.sharding import PartitionSpec as P

RATIOS = ((1, 1), (1, 2), (1, 4), (3, 4))
CHUNK = 256
LANES = 128


class Plan:
    def __init__(self, cols, taps, rows, owners):
        self.cols, self.taps, self.rows, self.owners = cols, taps, rows, owners
        self.granule = taps // 2
        self.held = cols // self.granule
        self.steps = [self.held * n // d for n, d in RATIOS]
        self.part_cols = [cols * n // d for n, d in RATIOS]
        self.part_rows = [rows * n // d for n, d in RATIOS]
        self.offsets, self.slots = [], []
        offset = slot = 0
        for width in self.part_cols:
            self.offsets.append(offset)
            self.slots.append(slot)
            offset += width + taps if self.offsets[1:] else 0
            slot += (width + taps) // self.granule
        self.width, self.slot_count = offset, slot

    def needs(self, to, source):
        first = self.held * source
        found = False
        for step in self.steps:
            found = found | ((step * (to + 1) >= first) & (step * to <= first + self.held))
        return found


def sends(plan, me):
    found = []
    for own in range(plan.held):
        for part, step in enumerate(plan.steps):
            spot = plan.held * me + own + 1
            last = spot // step
            rest = spot - last * step
            for back in range((step + 1) // step + 1):
                if plan.held % step == 0:
                    if (own + 1) % step + step * back >= step + 2:
                        continue
                to = last - back
                place = rest + step * back
                fits = (to >= 0) & (to < plan.owners) & (place < step + 2)
                found.append((own, part, to, place, fits))
    return found


def one_hot(shape, make):
    left = lax.broadcasted_iota(jnp.int32, shape, 0)
    right = lax.broadcasted_iota(jnp.int32, shape, 1)
    return make(left, right).astype(jnp.float32).astype(jnp.bfloat16)


def build(window, shifts, low, high):
    width = (high - low + 1) * LANES
    start = low * LANES
    bases = []

    def first(which):
        line = window[which : which + 1, start : start + width].astype(jnp.float32)
        base = jnp.broadcast_to(line, (8, width))
        place = lax.broadcasted_iota(jnp.int32, (8, width), 0)
        for bit in (1, 2, 4):
            base = jnp.where((place & bit) != 0, pltpu.roll(base, width - bit, 1), base)
        base = jnp.concatenate([base, pltpu.roll(base, width - 8, 1)], 0)
        bases.append(base.astype(jnp.bfloat16))

    def turned(which, turn):
        base = bases[which]
        into = shifts[which]
        moved = base if turn == 0 else pltpu.roll(base, width - 16 * turn, 1)
        for block in range(high - low):
            piece = moved[:, block * LANES : (block + 1) * LANES]
            spot = (low + block) * LANES + 16 * turn
            into[spot : spot + 16, 0:LANES] = piece
            if spot >= LANES:
                into[spot - LANES : spot - LANES + 16, LANES : 2 * LANES] = piece

    tasks = [functools.partial(first, which) for which in (0, 1)]
    tasks += [functools.partial(turned, which, turn) for turn in range(LANES // 16) for which in (0, 1)]
    return tasks


def power(lhs, shifts, count, taps, start, width):
    rows = lhs.shape[0] // 2
    if count == rows:
        left = lhs[...]
    else:
        left = jnp.concatenate([lhs[:count], lhs[rows : rows + count]], 0)
    right = jnp.concatenate(
        [
            jnp.concatenate(
                [shifts[which][start + at : start + at + taps, :] for at in range(0, width, CHUNK)], 1
            )
            for which in (0, 1)
        ],
        0,
    )
    both = jnp.dot(left, right, preferred_element_type=jnp.float32)
    real, imag = both[:count], both[count:]
    return (real * real + imag * imag).astype(jnp.bfloat16)


def gather_kernel(plan, spec_ref, index_ref, bank_ref, win_out, lhs_out, plane_out, win, bank, index, lhs, plane, *scratch):
    rows, taps, size = plan.rows, plan.taps, plan.granule
    parts = len(RATIOS)
    shifts = scratch[:2]
    bank_sem, index_sem, own_sem, out_sems, send_sems, recv_sems = scratch[2:]
    me = lax.axis_index("freq")

    own_start = size
    fetch_own = pltpu.make_async_copy(spec_ref, win.at[:, own_start : own_start + plan.cols], own_sem)
    fetch_own.start()
    fetch_index = pltpu.make_async_copy(index_ref, index, index_sem)
    fetch_index.start()
    fetch_bank = pltpu.make_async_copy(bank_ref, bank, bank_sem)
    fetch_bank.start()

    barrier = pltpu.get_barrier_semaphore()

    def greet(step, count):
        peer = lax.rem(me + step, plan.owners)
        met = plan.needs(me, peer) | plan.needs(peer, me)

        @pl.when(met)
        def _():
            pl.semaphore_signal(barrier, inc=1, device_id={"freq": peer}, device_id_type=pl.DeviceIdType.MESH)

        return count + jnp.where(met, 1, 0)

    partners = lax.fori_loop(1, plan.owners, greet, jnp.int32(0))

    @pl.when(me == 0)
    def _():
        win[:, 0:size] = jnp.zeros((2, size), win.dtype)

    @pl.when(me == plan.owners - 1)
    def _():
        end = plan.cols + plan.taps
        win[:, end - size : end] = jnp.zeros((2, size), win.dtype)

    def each(act_remote, act_local):
        for number, (own, part, to, place, fits) in enumerate(sends(plan, me)):
            source = spec_ref.at[:, own * size : (own + 1) * size]
            into = win if part == 0 else win_out
            target = into.at[:, pl.ds(pl.multiple_of(plan.offsets[part] + place * size, size), size)]
            got = recv_sems.at[plan.slots[part] + place]

            @pl.when(fits & (to != me))
            def _():
                act_remote(
                    pltpu.make_async_remote_copy(
                        src_ref=source,
                        dst_ref=target,
                        send_sem=send_sems.at[number],
                        recv_sem=got,
                        device_id={"freq": to},
                        device_id_type=pl.DeviceIdType.MESH,
                    )
                )

            if act_local is not None and part:

                @pl.when(fits & (to == me))
                def _():
                    act_local(pltpu.make_async_copy(source, target, got))

    def receive(part):
        step = plan.steps[part]
        for place in range(step + 2):
            if part == 0 and 0 < place <= plan.held:
                continue
            spot = step * me - 1 + place

            def land():
                start = plan.offsets[part] + place * size
                pltpu.make_async_copy(
                    spec_ref.at[:, 0:size],
                    (win if part == 0 else win_out).at[:, start : start + size],
                    recv_sems.at[plan.slots[part] + place],
                ).wait()

            if part:
                land()
            else:
                pl.when((spot >= 0) & (spot < plan.held * plan.owners))(land)

    def keep(chunk):
        plane[:, chunk * CHUNK : (chunk + 1) * CHUNK] = power(lhs, shifts, rows, taps, chunk * CHUNK, CHUNK)

    halo = size // LANES
    last = (plan.cols + taps) // LANES - 1

    fetch_own.wait()
    for task in build(win, shifts, halo, last - halo):
        task()
    fetch_index.wait()
    fetch_bank.wait()
    names = lax.broadcasted_iota(jnp.int32, (bank.shape[1], rows), 0)
    picks = (names == index[...]).astype(jnp.float32).T.astype(jnp.bfloat16)
    real = jnp.dot(picks, bank[0], preferred_element_type=jnp.float32).astype(jnp.bfloat16)
    imag = jnp.dot(picks, bank[1], preferred_element_type=jnp.float32).astype(jnp.bfloat16)
    lhs[:rows, :taps] = real
    lhs[rows:, :taps] = imag
    lhs[:rows, taps:] = -imag
    lhs[rows:, taps:] = real

    chunks = plan.cols // CHUNK
    edge = size // CHUNK
    for chunk in range(edge, chunks - edge):
        keep(chunk)
    put_lhs = pltpu.make_async_copy(lhs, lhs_out, out_sems.at[0])
    put_lhs.start()
    pl.semaphore_wait(barrier, partners)
    each(lambda copy: copy.start(), lambda copy: copy.start())

    @pl.when(me == 0)
    def _():
        for part in range(1, parts):
            start = plan.offsets[part]
            pltpu.make_async_copy(
                win.at[:, 0:size], win_out.at[:, start : start + size], recv_sems.at[plan.slots[part]]
            ).start()

    receive(0)
    for task in build(win, shifts, 0, halo) + build(win, shifts, last - halo, last):
        task()
    for chunk in [*range(edge), *range(chunks - edge, chunks)]:
        keep(chunk)
    put_plane = pltpu.make_async_copy(plane, plane_out, out_sems.at[1])
    put_plane.start()
    for part in range(1, parts):
        receive(part)
    put_lhs.wait()
    put_plane.wait()
    each(lambda copy: copy.wait_send(), None)


def search_kernel(plan, win_ref, lhs_ref, plane_ref, out_ref, win, lhs, plane, out, *scratch):
    rows, taps = plan.rows, plan.taps
    parts = len(RATIOS)
    shifts, held = scratch[: 2 * parts - 2], scratch[2 * parts - 2 : 3 * parts - 3]
    in_sems, out_sems = scratch[3 * parts - 3 :]
    offsets = plan.offsets
    fetch_win = pltpu.make_async_copy(win_ref, win, in_sems.at[0])
    fetch_lhs = pltpu.make_async_copy(lhs_ref, lhs, in_sems.at[1])
    fetch_plane = pltpu.make_async_copy(plane_ref, plane, in_sems.at[2])
    fetch_win.start()
    fetch_lhs.start()
    fetch_plane.start()

    def put(chunk):
        spot = slice(chunk * CHUNK, (chunk + 1) * CHUNK)
        return pltpu.make_async_copy(out.at[:, spot], out_ref.at[:, spot], out_sems.at[chunk])

    def fill(part, start):
        width = 2 * CHUNK
        n, d = RATIOS[part]
        spread = one_hot((rows, plan.part_rows[part]), lambda z, k: z * n // d == k)
        cells = jnp.dot(spread, power(lhs, shifts[2 * part - 2 : 2 * part], plan.part_rows[part], taps, start, width), preferred_element_type=jnp.float32)
        held[part - 1][:, start : start + width] = cells.astype(jnp.bfloat16)

    def finish(chunk):
        half = one_hot((LANES, CHUNK), lambda k, r: k == r // 2)
        quarters = [one_hot((LANES, CHUNK), lambda k, r: k == CHUNK // 4 * odd + r // 4) for odd in (0, 1)]
        threes = [one_hot((CHUNK, CHUNK), lambda k, r: k == CHUNK // 4 * odd + 3 * r // 4) for odd in (0, 1)]
        step, odd = divmod(chunk, 2)
        spots = (
            (held[0], chunk * LANES, half),
            (held[1], step * LANES, quarters[odd]),
            (held[2], (3 * step + odd) * LANES, threes[odd]),
        )
        cells = jnp.concatenate([ref[:, at : at + spread.shape[0]] for ref, at, spread in spots], 1)
        spreads = jnp.concatenate([spread for _, _, spread in spots], 0)
        total = plane[:, chunk * CHUNK : (chunk + 1) * CHUNK].astype(jnp.float32)
        total += jnp.dot(cells, spreads, preferred_element_type=jnp.float32)
        out[:, chunk * CHUNK : (chunk + 1) * CHUNK] = total
        put(chunk).start()

    def run(products, builds):
        done = 0
        for number, product in enumerate(products):
            product()
            until = len(builds) * (number + 1) // len(products)
            for task in builds[done:until]:
                task()
            done = until

    def fills(part):
        return [functools.partial(fill, part, start) for start in range(0, plan.part_cols[part], 2 * CHUNK)]

    def whole(part):
        return build(win.at[:, offsets[part] : offsets[part] + plan.part_cols[part] + taps], shifts[2 * part - 2 : 2 * part], 0, (plan.part_cols[part] + taps) // LANES - 1)

    fetch_win.wait()
    for task in whole(2):
        task()
    fetch_lhs.wait()
    run(fills(2), whole(1))
    run(fills(1), whole(3))
    run(fills(3), [])
    fetch_plane.wait()
    for chunk in range(plan.cols // CHUNK):
        finish(chunk)
    for chunk in range(plan.cols // CHUNK):
        put(chunk).wait()


def body(spectrum, template_bank, template_index):
    owners = lax.axis_size("freq")
    taps = template_bank.shape[2]
    rows = template_index.shape[0]
    cols = spectrum.shape[1]
    plan = Plan(cols, taps, rows, owners)
    hbm = pl.BlockSpec(memory_space=pl.ANY)
    between = (
        ((2, plan.width), jnp.bfloat16),
        ((2 * rows, 2 * taps), jnp.bfloat16),
        ((rows, cols), jnp.bfloat16),
    )
    windows, lhs, plane = pl.pallas_call(
        functools.partial(gather_kernel, plan),
        out_shape=tuple(jax.ShapeDtypeStruct(*item) for item in between),
        in_specs=[hbm] * 3,
        out_specs=(hbm,) * 3,
        scratch_shapes=[
            pltpu.VMEM((2, cols + taps), jnp.bfloat16),
            pltpu.VMEM(template_bank.shape, jnp.bfloat16),
            pltpu.VMEM((1, rows), jnp.int32),
            *[pltpu.VMEM(*item) for item in between[1:]],
            *[pltpu.VMEM((cols + taps, CHUNK), jnp.bfloat16) for _ in range(2)],
            pltpu.SemaphoreType.DMA,
            pltpu.SemaphoreType.DMA,
            pltpu.SemaphoreType.DMA,
            pltpu.SemaphoreType.DMA((2,)),
            pltpu.SemaphoreType.DMA((len(sends(plan, 0)),)),
            pltpu.SemaphoreType.DMA((plan.slot_count,)),
        ],
        compiler_params=pltpu.CompilerParams(collective_id=0, has_side_effects=True),
        name="gather",
    )(spectrum, template_index.reshape(1, rows), template_bank)
    return pl.pallas_call(
        functools.partial(search_kernel, plan),
        out_shape=jax.ShapeDtypeStruct((rows, cols), jnp.float32),
        in_specs=[hbm] * 3,
        out_specs=hbm,
        scratch_shapes=[
            *[pltpu.VMEM(*item) for item in between],
            pltpu.VMEM((rows, cols), jnp.float32),
            *[pltpu.VMEM((width + taps, CHUNK), jnp.bfloat16) for width in plan.part_cols[1:] for _ in range(2)],
            *[pltpu.VMEM((rows, width), jnp.bfloat16) for width in plan.part_cols[1:]],
            pltpu.SemaphoreType.DMA((3,)),
            pltpu.SemaphoreType.DMA((cols // CHUNK,)),
        ],
        name="search",
    )(windows, lhs, plane)


def solution(mesh):
    return jax.shard_map(
        body,
        mesh=mesh,
        in_specs=(P(None, ("beam", "freq")), P(), P()),
        out_specs=P(None, ("beam", "freq")),
        check_vma=False,
    )
```

```python
import functools

import jax
import jax.numpy as jnp
from jax import lax
from jax.experimental import pallas as pl
from jax.experimental.pallas import tpu as pltpu
from jax.sharding import PartitionSpec as P

RATIOS = ((1, 1), (1, 2), (1, 4), (3, 4))
CHUNK = 256
LANES = 128


class Plan:
    def __init__(self, cols, taps, rows, owners):
        self.cols, self.taps, self.rows, self.owners = cols, taps, rows, owners
        self.granule = taps // 2
        self.held = cols // self.granule
        self.steps = [self.held * n // d for n, d in RATIOS]
        self.part_cols = [cols * n // d for n, d in RATIOS]
        self.part_rows = [rows * n // d for n, d in RATIOS]
        self.offsets, self.slots = [], []
        offset = slot = 0
        for width in self.part_cols:
            self.offsets.append(offset)
            self.slots.append(slot)
            offset += width + taps if self.offsets[1:] else 0
            slot += (width + taps) // self.granule
        self.width, self.slot_count = offset, slot

    def needs(self, to, source):
        first = self.held * source
        found = False
        for step in self.steps:
            found = found | ((step * (to + 1) >= first) & (step * to <= first + self.held))
        return found


def sends(plan, me):
    found = []
    for own in range(plan.held):
        for part, step in enumerate(plan.steps):
            spot = plan.held * me + own + 1
            last = spot // step
            rest = spot - last * step
            for back in range((step + 1) // step + 1):
                if plan.held % step == 0:
                    if (own + 1) % step + step * back >= step + 2:
                        continue
                to = last - back
                place = rest + step * back
                fits = (to >= 0) & (to < plan.owners) & (place < step + 2)
                found.append((own, part, to, place, fits))
    return found


def one_hot(shape, make):
    left = lax.broadcasted_iota(jnp.int32, shape, 0)
    right = lax.broadcasted_iota(jnp.int32, shape, 1)
    return make(left, right).astype(jnp.float32).astype(jnp.bfloat16)


def build(window, shifts, low, high):
    width = (high - low + 1) * LANES
    start = low * LANES
    bases = []

    def first(which):
        line = window[which : which + 1, start : start + width].astype(jnp.float32)
        base = jnp.broadcast_to(line, (8, width))
        place = lax.broadcasted_iota(jnp.int32, (8, width), 0)
        for bit in (1, 2, 4):
            base = jnp.where((place & bit) != 0, pltpu.roll(base, width - bit, 1), base)
        base = jnp.concatenate([base, pltpu.roll(base, width - 8, 1)], 0)
        bases.append(base.astype(jnp.bfloat16))

    def turned(which, turn):
        base = bases[which]
        into = shifts[which]
        moved = base if turn == 0 else pltpu.roll(base, width - 16 * turn, 1)
        for block in range(high - low):
            piece = moved[:, block * LANES : (block + 1) * LANES]
            spot = (low + block) * LANES + 16 * turn
            into[spot : spot + 16, 0:LANES] = piece
            if spot >= LANES:
                into[spot - LANES : spot - LANES + 16, LANES : 2 * LANES] = piece

    tasks = [functools.partial(first, which) for which in (0, 1)]
    tasks += [functools.partial(turned, which, turn) for turn in range(LANES // 16) for which in (0, 1)]
    return tasks


def power(lhs, shifts, count, taps, start, width):
    rows = lhs.shape[0] // 2
    if count == rows:
        left = lhs[...]
    else:
        left = jnp.concatenate([lhs[:count], lhs[rows : rows + count]], 0)
    right = jnp.concatenate(
        [
            jnp.concatenate(
                [shifts[which][start + at : start + at + taps, :] for at in range(0, width, CHUNK)], 1
            )
            for which in (0, 1)
        ],
        0,
    )
    both = jnp.dot(left, right, preferred_element_type=jnp.float32)
    real, imag = both[:count], both[count:]
    return (real * real + imag * imag).astype(jnp.bfloat16)


def gather_kernel(plan, spec_ref, index_ref, bank_ref, win_out, lhs_out, plane_out, win, bank, index, lhs, plane, *scratch):
    rows, taps, size = plan.rows, plan.taps, plan.granule
    parts = len(RATIOS)
    shifts = scratch[:2]
    bank_sem, index_sem, own_sem, out_sems, send_sems, recv_sems = scratch[2:]
    me = lax.axis_index("freq")

    own_start = size
    fetch_own = pltpu.make_async_copy(spec_ref, win.at[:, own_start : own_start + plan.cols], own_sem)
    fetch_own.start()
    fetch_index = pltpu.make_async_copy(index_ref, index, index_sem)
    fetch_index.start()
    fetch_bank = pltpu.make_async_copy(bank_ref, bank, bank_sem)
    fetch_bank.start()

    barrier = pltpu.get_barrier_semaphore()

    def greet(step, carry):
        count, far = carry
        peer = lax.rem(me + step, plan.owners)
        met = plan.needs(me, peer) | plan.needs(peer, me)

        @pl.when(met)
        def _():
            pl.semaphore_signal(barrier, inc=1, device_id={"freq": peer}, device_id_type=pl.DeviceIdType.MESH)

        ahead = met & (peer - me >= 7 * plan.owners // 16)
        return count + jnp.where(met, 1, 0), far + jnp.where(ahead, 1, 0)

    partners, far = lax.fori_loop(1, plan.owners, greet, (jnp.int32(0), jnp.int32(0)))

    @pl.when(me == 0)
    def _():
        win[:, 0:size] = jnp.zeros((2, size), win.dtype)

    @pl.when(me == plan.owners - 1)
    def _():
        end = plan.cols + plan.taps
        win[:, end - size : end] = jnp.zeros((2, size), win.dtype)

    def each(act_remote, act_local):
        for number, (own, part, to, place, fits) in enumerate(sends(plan, me)):
            source = spec_ref.at[:, own * size : (own + 1) * size]
            into = win if part == 0 else win_out
            target = into.at[:, pl.ds(pl.multiple_of(plan.offsets[part] + place * size, size), size)]
            got = recv_sems.at[plan.slots[part] + place]

            @pl.when(fits & (to != me))
            def _():
                act_remote(
                    pltpu.make_async_remote_copy(
                        src_ref=source,
                        dst_ref=target,
                        send_sem=send_sems.at[number],
                        recv_sem=got,
                        device_id={"freq": to},
                        device_id_type=pl.DeviceIdType.MESH,
                    )
                )

            if act_local is not None and part:

                @pl.when(fits & (to == me))
                def _():
                    act_local(pltpu.make_async_copy(source, target, got))

    def receive(part):
        step = plan.steps[part]
        for place in range(step + 2):
            if part == 0 and 0 < place <= plan.held:
                continue
            spot = step * me - 1 + place

            def land():
                start = plan.offsets[part] + place * size
                pltpu.make_async_copy(
                    spec_ref.at[:, 0:size],
                    (win if part == 0 else win_out).at[:, start : start + size],
                    recv_sems.at[plan.slots[part] + place],
                ).wait()

            if part:
                land()
            else:
                pl.when((spot >= 0) & (spot < plan.held * plan.owners))(land)

    def keep(chunk):
        plane[:, chunk * CHUNK : (chunk + 1) * CHUNK] = power(lhs, shifts, rows, taps, chunk * CHUNK, CHUNK)

    halo = size // LANES
    last = (plan.cols + taps) // LANES - 1

    fetch_own.wait()
    for task in build(win, shifts, halo, last - halo):
        task()
    fetch_index.wait()
    fetch_bank.wait()
    names = lax.broadcasted_iota(jnp.int32, (bank.shape[1], rows), 0)
    picks = (names == index[...]).astype(jnp.float32).T.astype(jnp.bfloat16)
    real = jnp.dot(picks, bank[0], preferred_element_type=jnp.float32).astype(jnp.bfloat16)
    imag = jnp.dot(picks, bank[1], preferred_element_type=jnp.float32).astype(jnp.bfloat16)
    lhs[:rows, :taps] = real
    lhs[rows:, :taps] = imag
    lhs[:rows, taps:] = -imag
    lhs[rows:, taps:] = real

    chunks = plan.cols // CHUNK
    edge = size // CHUNK

    def interior():
        for chunk in range(edge, chunks - edge):
            keep(chunk)

    pl.when(far > 0)(interior)
    put_lhs = pltpu.make_async_copy(lhs, lhs_out, out_sems.at[0])
    put_lhs.start()
    pl.semaphore_wait(barrier, partners)
    each(lambda copy: copy.start(), lambda copy: copy.start())

    @pl.when(me == 0)
    def _():
        for part in range(1, parts):
            start = plan.offsets[part]
            pltpu.make_async_copy(
                win.at[:, 0:size], win_out.at[:, start : start + size], recv_sems.at[plan.slots[part]]
            ).start()

    pl.when(far == 0)(interior)
    receive(0)
    for task in build(win, shifts, 0, halo) + build(win, shifts, last - halo, last):
        task()
    for chunk in [*range(edge), *range(chunks - edge, chunks)]:
        keep(chunk)
    put_plane = pltpu.make_async_copy(plane, plane_out, out_sems.at[1])
    put_plane.start()
    for part in range(1, parts):
        receive(part)
    put_lhs.wait()
    put_plane.wait()
    each(lambda copy: copy.wait_send(), None)


def search_kernel(plan, win_ref, lhs_ref, plane_ref, out_ref, win, lhs, plane, out, *scratch):
    rows, taps = plan.rows, plan.taps
    parts = len(RATIOS)
    shifts, held = scratch[: 2 * parts - 2], scratch[2 * parts - 2 : 3 * parts - 3]
    in_sems, out_sems = scratch[3 * parts - 3 :]
    offsets = plan.offsets
    fetch_win = pltpu.make_async_copy(win_ref, win, in_sems.at[0])
    fetch_lhs = pltpu.make_async_copy(lhs_ref, lhs, in_sems.at[1])
    fetch_plane = pltpu.make_async_copy(plane_ref, plane, in_sems.at[2])
    fetch_win.start()
    fetch_lhs.start()
    fetch_plane.start()

    def put(chunk):
        spot = slice(chunk * CHUNK, (chunk + 1) * CHUNK)
        return pltpu.make_async_copy(out.at[:, spot], out_ref.at[:, spot], out_sems.at[chunk])

    def fill(part, start):
        width = 2 * CHUNK
        n, d = RATIOS[part]
        spread = one_hot((rows, plan.part_rows[part]), lambda z, k: z * n // d == k)
        cells = jnp.dot(spread, power(lhs, shifts[2 * part - 2 : 2 * part], plan.part_rows[part], taps, start, width), preferred_element_type=jnp.float32)
        held[part - 1][:, start : start + width] = cells.astype(jnp.bfloat16)

    def finish(chunk):
        half = one_hot((LANES, CHUNK), lambda k, r: k == r // 2)
        quarters = [one_hot((LANES, CHUNK), lambda k, r: k == CHUNK // 4 * odd + r // 4) for odd in (0, 1)]
        threes = [one_hot((CHUNK, CHUNK), lambda k, r: k == CHUNK // 4 * odd + 3 * r // 4) for odd in (0, 1)]
        step, odd = divmod(chunk, 2)
        spots = (
            (held[0], chunk * LANES, half),
            (held[1], step * LANES, quarters[odd]),
            (held[2], (3 * step + odd) * LANES, threes[odd]),
        )
        cells = jnp.concatenate([ref[:, at : at + spread.shape[0]] for ref, at, spread in spots], 1)
        spreads = jnp.concatenate([spread for _, _, spread in spots], 0)
        total = plane[:, chunk * CHUNK : (chunk + 1) * CHUNK].astype(jnp.float32)
        total += jnp.dot(cells, spreads, preferred_element_type=jnp.float32)
        out[:, chunk * CHUNK : (chunk + 1) * CHUNK] = total
        put(chunk).start()

    def run(products, builds):
        done = 0
        for number, product in enumerate(products):
            product()
            until = len(builds) * (number + 1) // len(products)
            for task in builds[done:until]:
                task()
            done = until

    def fills(part):
        return [functools.partial(fill, part, start) for start in range(0, plan.part_cols[part], 2 * CHUNK)]

    def whole(part):
        return build(win.at[:, offsets[part] : offsets[part] + plan.part_cols[part] + taps], shifts[2 * part - 2 : 2 * part], 0, (plan.part_cols[part] + taps) // LANES - 1)

    fetch_win.wait()
    for task in whole(2):
        task()
    fetch_lhs.wait()
    run(fills(2), whole(1))
    run(fills(1), whole(3))
    run(fills(3), [])
    fetch_plane.wait()
    for chunk in range(plan.cols // CHUNK):
        finish(chunk)
    for chunk in range(plan.cols // CHUNK):
        put(chunk).wait()


def body(spectrum, template_bank, template_index):
    owners = lax.axis_size("freq")
    taps = template_bank.shape[2]
    rows = template_index.shape[0]
    cols = spectrum.shape[1]
    plan = Plan(cols, taps, rows, owners)
    hbm = pl.BlockSpec(memory_space=pl.ANY)
    between = (
        ((2, plan.width), jnp.bfloat16),
        ((2 * rows, 2 * taps), jnp.bfloat16),
        ((rows, cols), jnp.bfloat16),
    )
    windows, lhs, plane = pl.pallas_call(
        functools.partial(gather_kernel, plan),
        out_shape=tuple(jax.ShapeDtypeStruct(*item) for item in between),
        in_specs=[hbm] * 3,
        out_specs=(hbm,) * 3,
        scratch_shapes=[
            pltpu.VMEM((2, cols + taps), jnp.bfloat16),
            pltpu.VMEM(template_bank.shape, jnp.bfloat16),
            pltpu.VMEM((1, rows), jnp.int32),
            *[pltpu.VMEM(*item) for item in between[1:]],
            *[pltpu.VMEM((cols + taps, CHUNK), jnp.bfloat16) for _ in range(2)],
            pltpu.SemaphoreType.DMA,
            pltpu.SemaphoreType.DMA,
            pltpu.SemaphoreType.DMA,
            pltpu.SemaphoreType.DMA((2,)),
            pltpu.SemaphoreType.DMA((len(sends(plan, 0)),)),
            pltpu.SemaphoreType.DMA((plan.slot_count,)),
        ],
        compiler_params=pltpu.CompilerParams(collective_id=0, has_side_effects=True),
        name="gather",
    )(spectrum, template_index.reshape(1, rows), template_bank)
    return pl.pallas_call(
        functools.partial(search_kernel, plan),
        out_shape=jax.ShapeDtypeStruct((rows, cols), jnp.float32),
        in_specs=[hbm] * 3,
        out_specs=hbm,
        scratch_shapes=[
            *[pltpu.VMEM(*item) for item in between],
            pltpu.VMEM((rows, cols), jnp.float32),
            *[pltpu.VMEM((width + taps, CHUNK), jnp.bfloat16) for width in plan.part_cols[1:] for _ in range(2)],
            *[pltpu.VMEM((rows, width), jnp.bfloat16) for width in plan.part_cols[1:]],
            pltpu.SemaphoreType.DMA((3,)),
            pltpu.SemaphoreType.DMA((cols // CHUNK,)),
        ],
        name="search",
    )(windows, lhs, plane)


def solution(mesh):
    return jax.shard_map(
        body,
        mesh=mesh,
        in_specs=(P(None, ("beam", "freq")), P(), P()),
        out_specs=P(None, ("beam", "freq")),
        check_vma=False,
    )
```

```python
import functools

import jax
import jax.numpy as jnp
from jax import lax
from jax.experimental import pallas as pl
from jax.experimental.pallas import tpu as pltpu
from jax.sharding import PartitionSpec as P

RATIOS = ((1, 1), (1, 2), (1, 4), (3, 4))
CHUNK = 256
LANES = 128


class Plan:
    def __init__(self, cols, taps, rows, owners):
        self.cols, self.taps, self.rows, self.owners = cols, taps, rows, owners
        self.granule = taps // 2
        self.held = cols // self.granule
        self.steps = [self.held * n // d for n, d in RATIOS]
        self.part_cols = [cols * n // d for n, d in RATIOS]
        self.part_rows = [rows * n // d for n, d in RATIOS]
        self.offsets, self.slots = [], []
        offset = slot = 0
        for width in self.part_cols:
            self.offsets.append(offset)
            self.slots.append(slot)
            offset += width + taps if self.offsets[1:] else 0
            slot += (width + taps) // self.granule
        self.width, self.slot_count = offset, slot

    def needs(self, to, source):
        first = self.held * source
        found = False
        for step in self.steps:
            found = found | ((step * (to + 1) >= first) & (step * to <= first + self.held))
        return found


def sends(plan, me):
    found = []
    for own in range(plan.held):
        for part, step in enumerate(plan.steps):
            spot = plan.held * me + own + 1
            last = spot // step
            rest = spot - last * step
            for back in range((step + 1) // step + 1):
                if plan.held % step == 0:
                    if (own + 1) % step + step * back >= step + 2:
                        continue
                to = last - back
                place = rest + step * back
                fits = (to >= 0) & (to < plan.owners) & (place < step + 2)
                found.append((own, part, to, place, fits))
    return found


def one_hot(shape, make):
    left = lax.broadcasted_iota(jnp.int32, shape, 0)
    right = lax.broadcasted_iota(jnp.int32, shape, 1)
    return make(left, right).astype(jnp.float32).astype(jnp.bfloat16)


def build(window, shifts, low, high):
    width = (high - low + 1) * LANES
    start = low * LANES
    bases = []

    def first(which):
        line = window[which : which + 1, start : start + width].astype(jnp.float32)
        base = jnp.broadcast_to(line, (8, width))
        place = lax.broadcasted_iota(jnp.int32, (8, width), 0)
        for bit in (1, 2, 4):
            base = jnp.where((place & bit) != 0, pltpu.roll(base, width - bit, 1), base)
        base = jnp.concatenate([base, pltpu.roll(base, width - 8, 1)], 0)
        bases.append(base.astype(jnp.bfloat16))

    def turned(which, turn):
        base = bases[which]
        into = shifts[which]
        moved = base if turn == 0 else pltpu.roll(base, width - 16 * turn, 1)
        for block in range(high - low):
            piece = moved[:, block * LANES : (block + 1) * LANES]
            spot = (low + block) * LANES + 16 * turn
            into[spot : spot + 16, 0:LANES] = piece
            if spot >= LANES:
                into[spot - LANES : spot - LANES + 16, LANES : 2 * LANES] = piece

    tasks = [functools.partial(first, which) for which in (0, 1)]
    tasks += [functools.partial(turned, which, turn) for turn in range(LANES // 16) for which in (0, 1)]
    return tasks


def power(lhs, shifts, count, taps, start, width):
    rows = lhs.shape[0] // 2
    if count == rows:
        left = lhs[...]
    else:
        left = jnp.concatenate([lhs[:count], lhs[rows : rows + count]], 0)
    right = jnp.concatenate(
        [
            jnp.concatenate(
                [shifts[which][start + at : start + at + taps, :] for at in range(0, width, CHUNK)], 1
            )
            for which in (0, 1)
        ],
        0,
    )
    both = jnp.dot(left, right, preferred_element_type=jnp.float32)
    real, imag = both[:count], both[count:]
    return (real * real + imag * imag).astype(jnp.bfloat16)


def gather_kernel(plan, spec_ref, index_ref, bank_ref, win_out, lhs_out, plane_out, win, bank, index, lhs, plane, *scratch):
    rows, taps, size = plan.rows, plan.taps, plan.granule
    parts = len(RATIOS)
    shifts = scratch[:2]
    bank_sem, index_sem, own_sem, out_sems, send_sems, recv_sems = scratch[2:]
    me = lax.axis_index("freq")

    own_start = size
    fetch_own = pltpu.make_async_copy(spec_ref, win.at[:, own_start : own_start + plan.cols], own_sem)
    fetch_own.start()
    fetch_index = pltpu.make_async_copy(index_ref, index, index_sem)
    fetch_index.start()
    fetch_bank = pltpu.make_async_copy(bank_ref, bank, bank_sem)
    fetch_bank.start()

    barrier = pltpu.get_barrier_semaphore()

    def greet(step, carry):
        count, far = carry
        peer = lax.rem(me + step, plan.owners)
        met = plan.needs(me, peer) | plan.needs(peer, me)

        @pl.when(met)
        def _():
            pl.semaphore_signal(barrier, inc=1, device_id={"freq": peer}, device_id_type=pl.DeviceIdType.MESH)

        ahead = met & (peer - me >= 7 * plan.owners // 16)
        return count + jnp.where(met, 1, 0), far + jnp.where(ahead, 1, 0)

    partners, far = lax.fori_loop(1, plan.owners, greet, (jnp.int32(0), jnp.int32(0)))

    @pl.when(me == 0)
    def _():
        win[:, 0:size] = jnp.zeros((2, size), win.dtype)

    @pl.when(me == plan.owners - 1)
    def _():
        end = plan.cols + plan.taps
        win[:, end - size : end] = jnp.zeros((2, size), win.dtype)

    def each(act_remote, act_local):
        for number, (own, part, to, place, fits) in enumerate(sends(plan, me)):
            source = spec_ref.at[:, own * size : (own + 1) * size]
            into = win if part == 0 else win_out
            target = into.at[:, pl.ds(pl.multiple_of(plan.offsets[part] + place * size, size), size)]
            got = recv_sems.at[plan.slots[part] + place]

            @pl.when(fits & (to != me))
            def _():
                act_remote(
                    pltpu.make_async_remote_copy(
                        src_ref=source,
                        dst_ref=target,
                        send_sem=send_sems.at[number],
                        recv_sem=got,
                        device_id={"freq": to},
                        device_id_type=pl.DeviceIdType.MESH,
                    )
                )

            if act_local is not None and part:

                @pl.when(fits & (to == me))
                def _():
                    act_local(pltpu.make_async_copy(source, target, got))

    def receive(part):
        step = plan.steps[part]
        for place in range(step + 2):
            if part == 0 and 0 < place <= plan.held:
                continue
            spot = step * me - 1 + place

            def land():
                start = plan.offsets[part] + place * size
                pltpu.make_async_copy(
                    spec_ref.at[:, 0:size],
                    (win if part == 0 else win_out).at[:, start : start + size],
                    recv_sems.at[plan.slots[part] + place],
                ).wait()

            if part:
                land()
            else:
                pl.when((spot >= 0) & (spot < plan.held * plan.owners))(land)

    def keep(chunk):
        plane[:, chunk * CHUNK : (chunk + 2) * CHUNK] = power(lhs, shifts, rows, taps, chunk * CHUNK, 2 * CHUNK)

    halo = size // LANES
    last = (plan.cols + taps) // LANES - 1

    fetch_own.wait()
    for task in build(win, shifts, halo, last - halo):
        task()
    fetch_index.wait()
    fetch_bank.wait()
    names = lax.broadcasted_iota(jnp.int32, (bank.shape[1], rows), 0)
    picks = (names == index[...]).astype(jnp.float32).T.astype(jnp.bfloat16)
    real = jnp.dot(picks, bank[0], preferred_element_type=jnp.float32).astype(jnp.bfloat16)
    imag = jnp.dot(picks, bank[1], preferred_element_type=jnp.float32).astype(jnp.bfloat16)
    lhs[:rows, :taps] = real
    lhs[rows:, :taps] = imag
    lhs[:rows, taps:] = -imag
    lhs[rows:, taps:] = real

    chunks = plan.cols // CHUNK
    edge = size // CHUNK

    def interior():
        for chunk in range(edge, chunks - edge, 2):
            keep(chunk)

    pl.when(far > 0)(interior)
    put_lhs = pltpu.make_async_copy(lhs, lhs_out, out_sems.at[0])
    put_lhs.start()
    pl.semaphore_wait(barrier, partners)
    each(lambda copy: copy.start(), lambda copy: copy.start())

    @pl.when(me == 0)
    def _():
        for part in range(1, parts):
            start = plan.offsets[part]
            pltpu.make_async_copy(
                win.at[:, 0:size], win_out.at[:, start : start + size], recv_sems.at[plan.slots[part]]
            ).start()

    pl.when(far == 0)(interior)
    receive(0)
    for task in build(win, shifts, 0, halo) + build(win, shifts, last - halo, last):
        task()
    for chunk in [*range(0, edge, 2), *range(chunks - edge, chunks, 2)]:
        keep(chunk)
    put_plane = pltpu.make_async_copy(plane, plane_out, out_sems.at[1])
    put_plane.start()
    for part in range(1, parts):
        receive(part)
    put_lhs.wait()
    put_plane.wait()
    each(lambda copy: copy.wait_send(), None)


def search_kernel(plan, win_ref, lhs_ref, plane_ref, out_ref, win, lhs, plane, out, *scratch):
    rows, taps = plan.rows, plan.taps
    parts = len(RATIOS)
    shifts, held = scratch[: 2 * parts - 2], scratch[2 * parts - 2 : 3 * parts - 3]
    in_sems, out_sems = scratch[3 * parts - 3 :]
    offsets = plan.offsets
    fetch_win = pltpu.make_async_copy(win_ref, win, in_sems.at[0])
    fetch_lhs = pltpu.make_async_copy(lhs_ref, lhs, in_sems.at[1])
    fetch_plane = pltpu.make_async_copy(plane_ref, plane, in_sems.at[2])
    fetch_win.start()
    fetch_lhs.start()
    fetch_plane.start()

    def put(chunk):
        spot = slice(chunk * CHUNK, (chunk + 1) * CHUNK)
        return pltpu.make_async_copy(out.at[:, spot], out_ref.at[:, spot], out_sems.at[chunk])

    def fill(part, start):
        width = 2 * CHUNK
        n, d = RATIOS[part]
        spread = one_hot((rows, plan.part_rows[part]), lambda z, k: z * n // d == k)
        cells = jnp.dot(spread, power(lhs, shifts[2 * part - 2 : 2 * part], plan.part_rows[part], taps, start, width), preferred_element_type=jnp.float32)
        held[part - 1][:, start : start + width] = cells.astype(jnp.bfloat16)

    def finish(chunk):
        half = one_hot((LANES, CHUNK), lambda k, r: k == r // 2)
        quarters = [one_hot((LANES, CHUNK), lambda k, r: k == CHUNK // 4 * odd + r // 4) for odd in (0, 1)]
        threes = [one_hot((CHUNK, CHUNK), lambda k, r: k == CHUNK // 4 * odd + 3 * r // 4) for odd in (0, 1)]
        step, odd = divmod(chunk, 2)
        spots = (
            (held[0], chunk * LANES, half),
            (held[1], step * LANES, quarters[odd]),
            (held[2], (3 * step + odd) * LANES, threes[odd]),
        )
        cells = jnp.concatenate([ref[:, at : at + spread.shape[0]] for ref, at, spread in spots], 1)
        spreads = jnp.concatenate([spread for _, _, spread in spots], 0)
        total = plane[:, chunk * CHUNK : (chunk + 1) * CHUNK].astype(jnp.float32)
        total += jnp.dot(cells, spreads, preferred_element_type=jnp.float32)
        out[:, chunk * CHUNK : (chunk + 1) * CHUNK] = total
        put(chunk).start()

    def run(products, builds):
        done = 0
        for number, product in enumerate(products):
            product()
            until = len(builds) * (number + 1) // len(products)
            for task in builds[done:until]:
                task()
            done = until

    def fills(part):
        return [functools.partial(fill, part, start) for start in range(0, plan.part_cols[part], 2 * CHUNK)]

    def whole(part):
        return build(win.at[:, offsets[part] : offsets[part] + plan.part_cols[part] + taps], shifts[2 * part - 2 : 2 * part], 0, (plan.part_cols[part] + taps) // LANES - 1)

    fetch_win.wait()
    for task in whole(2):
        task()
    fetch_lhs.wait()
    run(fills(2), whole(1))
    run(fills(1), whole(3))
    run(fills(3), [])
    fetch_plane.wait()
    for chunk in range(plan.cols // CHUNK):
        finish(chunk)
    for chunk in range(plan.cols // CHUNK):
        put(chunk).wait()


def body(spectrum, template_bank, template_index):
    owners = lax.axis_size("freq")
    taps = template_bank.shape[2]
    rows = template_index.shape[0]
    cols = spectrum.shape[1]
    plan = Plan(cols, taps, rows, owners)
    hbm = pl.BlockSpec(memory_space=pl.ANY)
    between = (
        ((2, plan.width), jnp.bfloat16),
        ((2 * rows, 2 * taps), jnp.bfloat16),
        ((rows, cols), jnp.bfloat16),
    )
    windows, lhs, plane = pl.pallas_call(
        functools.partial(gather_kernel, plan),
        out_shape=tuple(jax.ShapeDtypeStruct(*item) for item in between),
        in_specs=[hbm] * 3,
        out_specs=(hbm,) * 3,
        scratch_shapes=[
            pltpu.VMEM((2, cols + taps), jnp.bfloat16),
            pltpu.VMEM(template_bank.shape, jnp.bfloat16),
            pltpu.VMEM((1, rows), jnp.int32),
            *[pltpu.VMEM(*item) for item in between[1:]],
            *[pltpu.VMEM((cols + taps, CHUNK), jnp.bfloat16) for _ in range(2)],
            pltpu.SemaphoreType.DMA,
            pltpu.SemaphoreType.DMA,
            pltpu.SemaphoreType.DMA,
            pltpu.SemaphoreType.DMA((2,)),
            pltpu.SemaphoreType.DMA((len(sends(plan, 0)),)),
            pltpu.SemaphoreType.DMA((plan.slot_count,)),
        ],
        compiler_params=pltpu.CompilerParams(collective_id=0, has_side_effects=True),
        name="gather",
    )(spectrum, template_index.reshape(1, rows), template_bank)
    return pl.pallas_call(
        functools.partial(search_kernel, plan),
        out_shape=jax.ShapeDtypeStruct((rows, cols), jnp.float32),
        in_specs=[hbm] * 3,
        out_specs=hbm,
        scratch_shapes=[
            *[pltpu.VMEM(*item) for item in between],
            pltpu.VMEM((rows, cols), jnp.float32),
            *[pltpu.VMEM((width + taps, CHUNK), jnp.bfloat16) for width in plan.part_cols[1:] for _ in range(2)],
            *[pltpu.VMEM((rows, width), jnp.bfloat16) for width in plan.part_cols[1:]],
            pltpu.SemaphoreType.DMA((3,)),
            pltpu.SemaphoreType.DMA((cols // CHUNK,)),
        ],
        name="search",
    )(windows, lhs, plane)


def solution(mesh):
    return jax.shard_map(
        body,
        mesh=mesh,
        in_specs=(P(None, ("beam", "freq")), P(), P()),
        out_specs=P(None, ("beam", "freq")),
        check_vma=False,
    )
```
